512 devices in a mesh: pipe: 16 (over z), hid: 32 (over x, y, core).
Axes of the slice: x: 4, y: 4, z: 16, core: 2. Of those that a mesh axis runs over, the one named last changes fastest.
Arguments:
- section_inputs: bfloat16 [16, 3, 256, 1024], P('pipe', None, 'hid'), may hold values from -6 to 6
- w_in: bfloat16 [16, 1024, 32768], P('pipe', None, 'hid'), may hold values from -0.1875 to 0.1875
- w_out: bfloat16 [16, 32768, 1024], P('pipe', 'hid'), may hold values from -0.03125 to 0.03125
- warm_factor: float32 [16, 1024, 16], P('pipe'), may hold values from -6 to 6
- pending_left: float32 [16, 256, 16], P('pipe'), may hold values from -0.375 to 0.375
- pending_right: float32 [16, 1024, 16], P('pipe'), may hold values from -24 to 24
- incoming_left: float32 [3, 256, 16], replicated, may hold values from -0.375 to 0.375
- incoming_right: float32 [3, 1024, 16], replicated, may hold values from -24 to 24
Outputs:
- section_grads: float32 [16, 256, 1024], P('pipe', 'hid')
- final_left: float32 [16, 256, 16], P('pipe', 'hid')
- final_right: float32 [16, 1024, 16], P('pipe')
The draws below stay inside these ranges and needn't reach their ends.
All inputs are finite; a program needn't handle non-finite values.
Results may differ from the reference program's by a relative error of at most 0.02.
Values may be sent and summed in bfloat16 or wider, within the bound.
A program may use at most 64 MiB of HBM per device.

```python
import jax
import jax.numpy as jnp
from jax import lax

D = 1024
FF = 32768
RANK = 16
TICKS = 3
ROWS = 256
SECTIONS = 16


def factor_entries(key, shape, scale):
    values = jax.random.truncated_normal(key, -6.0, 6.0, shape, jnp.float32)
    return values * scale


def draw_warm_factor(key, part):
    return factor_entries(jax.random.fold_in(key, 11), (SECTIONS, D, RANK), 1.0)


def draw_pending_left(key, part):
    return factor_entries(jax.random.fold_in(key, 12), (SECTIONS, ROWS, RANK), 0.0625)


def draw_pending_right(key, part):
    return factor_entries(jax.random.fold_in(key, 13), (SECTIONS, D, RANK), 4.0)


def draw_incoming_left(key, part):
    return factor_entries(jax.random.fold_in(key, 14), (TICKS, ROWS, RANK), 0.0625)


def draw_incoming_right(key, part):
    return factor_entries(jax.random.fold_in(key, 15), (TICKS, D, RANK), 4.0)


def block_scale(stream_key, shape, shards, smallest, largest):
    level, own = 1.0, jax.random.fold_in(stream_key, 6)
    for position, parts in shards:
        steps = jnp.exp(jax.random.uniform(jax.random.fold_in(own, position), (parts,), jnp.float32, smallest / len(shards), largest / len(shards)))
        level = level * jnp.repeat(steps, shape[position] // parts).reshape([-1 if axis == position else 1 for axis in range(len(shape))])
    return level


def noise(stream_key, dims, scale, reach, split=(), kind=jnp.bfloat16):
    result = scale * jax.random.normal(stream_key, dims, jnp.float32)
    if split:
        result = result * block_scale(stream_key, dims, split, -0.22, 0.18)
    return jnp.clip(result, -reach, reach).astype(kind)


def setup_inputs(seed: int = 0) -> dict:
    key_list = jax.random.split(jax.random.key(seed), 9)
    return {
        "section_inputs": noise(key_list[0], (SECTIONS, TICKS, ROWS, D), 1.0, 6.0, ((0, 16), (2, 32))),
        "w_in": noise(key_list[1], (SECTIONS, D, FF), D ** -0.5, 0.1875, ((0, 16), (2, 32))),
        "w_out": noise(key_list[2], (SECTIONS, FF, D), FF ** -0.5, 0.03125, ((0, 16), (1, 32))),
        "warm_factor": draw_warm_factor(jax.random.fold_in(key_list[8], 71), 0),
        "pending_left": draw_pending_left(jax.random.fold_in(key_list[8], 71), 0),
        "pending_right": draw_pending_right(jax.random.fold_in(key_list[8], 71), 0),
        "incoming_left": draw_incoming_left(jax.random.fold_in(key_list[8], 71), 0),
        "incoming_right": draw_incoming_right(jax.random.fold_in(key_list[8], 71), 0),
    }


def orthonormal(merged, warm_basis):
    projected = jnp.dot(merged.astype(jnp.float32), warm_basis.astype(jnp.float32), precision=lax.Precision.HIGHEST, preferred_element_type=jnp.float32)
    gram_matrix = jnp.dot(projected.T.astype(jnp.float32), projected.astype(jnp.float32), precision=lax.Precision.HIGHEST, preferred_element_type=jnp.float32)
    lower_factor = jnp.linalg.cholesky(gram_matrix)
    new_left = jax.scipy.linalg.solve_triangular(lower_factor, projected.T, lower=True).T
    new_right = jnp.dot(merged.T.astype(jnp.float32), new_left.astype(jnp.float32), precision=lax.Precision.HIGHEST, preferred_element_type=jnp.float32)
    return (new_left, new_right)

def per_section(section_items):
    inputs_now, w_in_section, w_out_section, left_factor, right_factor, warm_basis = section_items
    cotangent = jnp.dot(left_factor.astype(jnp.float32), right_factor.T.astype(jnp.float32), precision=lax.Precision.HIGHEST, preferred_element_type=jnp.float32)
    cotangent_low = cotangent.astype(jnp.bfloat16)
    upward = jnp.dot(cotangent_low.astype(jnp.float32), w_out_section.T.astype(jnp.float32), preferred_element_type=jnp.float32)
    preact = jnp.dot(inputs_now.astype(jnp.float32), w_in_section.astype(jnp.float32), preferred_element_type=jnp.float32)
    hidden_grad = jnp.where(preact > 0, upward, jnp.zeros_like(upward)).astype(jnp.bfloat16)
    merged = cotangent + jnp.dot(hidden_grad.astype(jnp.float32), w_in_section.T.astype(jnp.float32), preferred_element_type=jnp.float32)
    new_left, new_right = orthonormal(merged, warm_basis)
    return (merged, new_left, new_right)

def reference(section_inputs, w_in, w_out, warm_factor, pending_left, pending_right, incoming_left, incoming_right):
    held_left = pending_left
    held_right = pending_right
    warm_basis = warm_factor
    merged = None
    new_left = None
    new_right = None
    for tick_index in range(TICKS):
        left_all = jnp.concatenate([held_left[:-1], incoming_left[tick_index][None]], 0)
        right_all = jnp.concatenate([held_right[:-1], incoming_right[tick_index][None]], 0)
        merged, new_left, new_right = lax.map(per_section, (section_inputs[:, tick_index], w_in, w_out, left_all, right_all, warm_basis))
        held_left = jnp.concatenate([new_left[1:], jnp.zeros_like(new_left[:1])], 0)
        held_right = jnp.concatenate([new_right[1:], jnp.zeros_like(new_right[:1])], 0)
        warm_basis = new_right
    return (merged, new_left, new_right)
```

```python
import jax
import jax.numpy as jnp
from jax import lax
from jax.experimental import pallas as pl
from jax.experimental.pallas import tpu as pltpu
from jax.sharding import PartitionSpec as P

MESH = pl.DeviceIdType.MESH
F32 = jnp.float32
BF16 = jnp.bfloat16
TICKS = 3
NX, NY, NC = 4, 4, 2
CHIPS = NX * NY
RANK = 16
ROWS = 256
D = 1024
LANES = 128
PIECES = D // LANES
OWN = ROWS // (CHIPS * NC)


def split(value):
    high = value.astype(BF16)
    low = (value - high.astype(F32)).astype(BF16)
    return high, low


def mm(first, second, dims=((1,), (0,))):
    return lax.dot_general(first, second, (dims, ((), ())), preferred_element_type=F32)


def mm_high(first, second, dims=((1,), (0,))):
    return lax.dot_general(
        first,
        second,
        (dims, ((), ())),
        precision=lax.Precision.HIGHEST,
        preferred_element_type=F32,
    )


def thin(value, matrix, dims):
    high, low = split(value)
    both = mm(jnp.concatenate([high, low], axis=0), matrix, dims)
    return both[:RANK] + both[RANK:]


def inverse_lower(gram):
    row = lax.broadcasted_iota(jnp.int32, (RANK, LANES), 0)
    lane = lax.broadcasted_iota(jnp.int32, (RANK, LANES), 1)
    work = jnp.concatenate([gram, jnp.zeros((RANK, LANES - RANK), F32)], axis=1)
    work = work + jnp.where(lane == row + RANK, 1.0, 0.0).astype(F32)
    pivots = jnp.zeros((RANK, LANES), F32)
    for k in range(RANK):
        column = jnp.broadcast_to(work[:, k : k + 1], (RANK, LANES))
        pivot = jnp.broadcast_to(column[k : k + 1, :], (RANK, LANES))
        along = jnp.broadcast_to(work[k : k + 1, :], (RANK, LANES))
        factor = jnp.where(row > k, column / pivot, 0.0)
        work = work - factor * along
        pivots = jnp.where(row == k, pivot, pivots)
    scaled = work * lax.rsqrt(pivots)
    return scaled[:, RANK : 2 * RANK]


def kernel(
    x_hbm,
    wi_hbm,
    wo_hbm,
    warm_hbm,
    pend_l_hbm,
    pend_r_hbm,
    inc_l_hbm,
    inc_r_hbm,
    grads_out,
    left_out,
    right_out,
    wi,
    wo,
    x_full,
    mask,
    hg,
    l_f32,
    r_f32,
    b_f32,
    l_inc,
    r_inc,
    ps,
    pbuf1,
    ps1,
    pbuf2,
    zs,
    zbuf1,
    zs1,
    zbuf2,
    rp,
    rbuf,
    rzbuf,
    ls,
    lz,
    rows_f32,
    mfull,
    msend,
    mpair,
    mpart,
    mbuf,
    local_sem,
    ag_send,
    ag_recv,
    agp_send,
    agp_recv,
    p1_send,
    p1_recv,
    p2_send,
    p2_recv,
    z1_send,
    z1_recv,
    z2_send,
    z2_recv,
    r_send,
    r_recv,
    rz_send,
    rz_recv,
    l_send,
    l_recv,
    m_send,
    m_recv,
):
    s = lax.axis_index("pipe")
    last_section = lax.axis_size("pipe") - 1
    h = lax.axis_index("hid")
    chip = h // NC
    c = h % NC
    x = chip // NY
    y = chip % NY
    oc = 1 - c
    xs = [x] + [(x + o) % NX for o in range(1, NX)]
    ys = [y] + [(y + o) % NY for o in range(1, NY)]
    cs = [c, oc]
    g1 = x * NC + c
    is_top = s == last_section
    has_above = s < last_section
    has_below = s > 0
    far = (2, 1, 3)
    group = [(o, e) for o in far for e in range(NC)] + [(0, 1)]
    chips = [(i, j) for i in (2, 1, 3, 0) for j in (2, 1, 3, 0) if (i, j) != (0, 0)]

    def hid(xx, yy, cc):
        return xx * (NY * NC) + yy * NC + cc

    def send(src, dst, send_sem, recv_sem, target):
        pltpu.make_async_remote_copy(
            src_ref=src,
            dst_ref=dst,
            send_sem=send_sem,
            recv_sem=recv_sem,
            device_id=target,
            device_id_type=MESH,
        ).start()

    def drain(ref, sem, name="out"):
        with jax.named_scope(name):
            pltpu.make_async_copy(ref, ref, sem).wait()

    barrier = pltpu.get_barrier_semaphore()

    def signal(target):
        pl.semaphore_signal(barrier, inc=1, device_id=target, device_id_type=MESH)

    for i, j in chips:
        signal((s, hid(xs[i], ys[j], c)))

    @pl.when(has_below)
    def _():
        for i in range(NX):
            for e in range(NC):
                signal((s - 1, hid(xs[i], y, cs[e])))

    @pl.when(has_above)
    def _():
        for i in range(NX):
            for e in range(NC):
                signal((s + 1, hid(xs[i], y, cs[e])))

    for o in far:
        signal((s, hid(xs[o], y, oc)))
        signal((s, hid(x, ys[o], oc)))
    signal((s, hid(x, y, oc)))

    own_x = [
        pltpu.make_async_copy(x_hbm.at[t], x_full.at[t, chip, c], ag_recv.at[t, 0])
        for t in range(TICKS)
    ]
    for copy in own_x:
        copy.start()
    loads = [
        pltpu.make_async_copy(warm_hbm, b_f32, local_sem.at[0]),
        pltpu.make_async_copy(inc_l_hbm, l_inc, local_sem.at[3]),
        pltpu.make_async_copy(inc_r_hbm, r_inc, local_sem.at[4]),
        pltpu.make_async_copy(pend_l_hbm, l_f32, local_sem.at[5]),
        pltpu.make_async_copy(pend_r_hbm, r_f32, local_sem.at[6]),
        pltpu.make_async_copy(wo_hbm, wo, local_sem.at[1]),
        pltpu.make_async_copy(wi_hbm, wi, local_sem.at[2]),
    ]
    for load in loads:
        load.start()

    neighbours = has_below.astype(jnp.int32) + has_above.astype(jnp.int32)
    with jax.named_scope("entry"):
        pl.semaphore_wait(barrier, CHIPS + 2 * (NX - 1) + NX * NC * neighbours)

    def gather_rows(t, targets):
        for i, j in targets:
            send(
                x_hbm.at[t],
                x_full.at[t, chip, c],
                ag_send.at[t],
                ag_recv.at[t, (NX - i) % NX],
                (s, hid(xs[i], ys[j], c)),
            )

    def share_rows(t):
        for i in (0, 1, 3, 2):
            four = x_full.at[t, pl.ds(xs[i] * NY, NY), c]
            drain(four, ag_recv.at[t, i], "ag_recv")
            send(four, four, agp_send.at[t], agp_recv.at[t], (s, hid(x, y, oc)))

    def make_mask(t):
        drain(x_full.at[t, :, oc], agp_recv.at[t], "agp_recv")
        with jax.named_scope("mask"):
            rows = x_full[t].reshape(ROWS, D)
            preact = mm(rows, wi[...])
            mask[...] = jnp.where(preact > 0, 1.0, 0.0).astype(BF16)

    def scatter_merged(targets):
        for i, j in targets:
            send(
                mpart.at[xs[i] * NY + ys[j]],
                mbuf.at[chip],
                m_send.at[1],
                m_recv.at[1],
                (s, hid(xs[i], ys[j], c)),
            )

    def low_cotangent():
        l_high, l_low = split(l_f32[...])
        r_high, r_low = split(r_f32[...])
        l_three = jnp.concatenate([l_high, l_high, l_low], axis=0)
        r_three = jnp.concatenate([r_high, r_low, r_high], axis=0)
        return mm(l_three, r_three, ((0,), (0,))).astype(BF16)

    gather_rows(0, chips)
    with jax.named_scope("loads"):
        for load in loads:
            load.wait()

    @pl.when(is_top)
    def _():
        l_f32[...] = l_inc[0]
        r_f32[...] = r_inc[0]

    for t in range(TICKS):
        last = t + 1 == TICKS
        if t > 0:
            drain(rbuf.at[t - 1, pl.ds(0, NX * NC - 1)], r_recv.at[t - 1], "r_recv")
            for j in range(PIECES):
                b_f32[:, j * LANES : (j + 1) * LANES] = rbuf[t - 1, j]
        with jax.named_scope("v"):
            v = thin(b_f32[...], wi[...], ((1,), (0,)))
        if t > 0:

            @pl.when(has_above)
            def _():
                drain(lz.at[t - 1], l_recv.at[t - 1], "l_recv")
                l_f32[...] = lz[t - 1]
                drain(rzbuf.at[t - 1], rz_recv.at[t - 1], "rz_recv")
                for j in range(PIECES):
                    r_f32[:, j * LANES : (j + 1) * LANES] = rzbuf[t - 1, j]

            @pl.when(is_top)
            def _():
                l_f32[...] = l_inc[t]
                r_f32[...] = r_inc[t]

        with jax.named_scope("upward"):
            upward = mm(low_cotangent(), wo[...], ((1,), (1,)))
            if t > 0:
                hg[...] = upward.astype(BF16) * mask[...]
            else:
                hg[...] = upward.astype(BF16)
        if t == 0:
            share_rows(0)
            make_mask(0)
            hg[...] = hg[...] * mask[...]
        with jax.named_scope("p_part"):
            p_part = thin(v, hg[...], ((1,), (1,)))
            ps[t, 0] = p_part[:, :LANES]
            ps[t, 1] = p_part[:, LANES:]
        for o, e in group:
            send(
                ps.at[t, cs[e]],
                pbuf1.at[t, g1],
                p1_send.at[t],
                p1_recv.at[t],
                (s, hid(xs[o], y, cs[e])),
            )
        pbuf1[t, g1] = ps[t, c]
        if not last:
            gather_rows(t + 1, chips[:5])
        with jax.named_scope("p_cot"):
            cross = mm_high(b_f32[...], r_f32[...], ((1,), (1,)))
            p_cot = mm_high(cross, l_f32[...])
        if last:
            with jax.named_scope("merged"):
                mfull[...] = mm(hg[...], wi[...], ((1,), (1,)))
                for k in range(CHIPS):
                    for e in range(NC):
                        base = (k * NC + e) * OWN
                        msend[e, k] = mfull[base : base + OWN, :].astype(BF16)
            send(
                msend.at[oc],
                mpair,
                m_send.at[0],
                m_recv.at[0],
                (s, hid(x, y, oc)),
            )
        drain(pbuf1.at[t, pl.ds(0, NX * NC - 1)], p1_recv.at[t], "p1_recv")
        p_sum = pbuf1[t, 0]
        for j in range(1, NX * NC):
            p_sum = p_sum + pbuf1[t, j]
        ps1[t] = p_sum
        for o, e in group:
            send(
                ps1.at[t],
                pbuf2.at[t, c * NY + y],
                p2_send.at[t],
                p2_recv.at[t],
                (s, hid(x, ys[o], cs[e])),
            )
        pbuf2[t, c * NY + y] = p_sum
        if last:
            drain(mpair, m_recv.at[0], "m_recv")
            with jax.named_scope("mpart"):
                mpart[...] = (msend[c].astype(F32) + mpair[...].astype(F32)).astype(BF16)
            scatter_merged(chips[:5])
            mbuf[chip] = mpart[chip]
        else:
            gather_rows(t + 1, chips[5:10])
        drain(pbuf2.at[t, pl.ds(0, NY * NC - 1)], p2_recv.at[t], "p2_recv")
        with jax.named_scope("z_part"):
            halves = []
            for e in range(NC):
                half = pbuf2[t, e * NY]
                for j in range(1, NY):
                    half = half + pbuf2[t, e * NY + j]
                halves.append(half)
            projected = jnp.concatenate(halves, axis=1) + p_cot
            y_part = thin(projected, hg[...], ((1,), (0,)))
            z_part = thin(y_part, wi[...], ((1,), (1,)))
            for j in range(PIECES):
                zs[t, j] = z_part[:, j * LANES : (j + 1) * LANES]
        for o, e in group:
            j = xs[o] * NC + cs[e]
            send(
                zs.at[t, j],
                zbuf1.at[t, g1],
                z1_send.at[t],
                z1_recv.at[t],
                (s, hid(xs[o], y, cs[e])),
            )
        zbuf1[t, g1] = zs[t, g1]
        if last:
            scatter_merged(chips[5:10])
        else:
            gather_rows(t + 1, chips[10:])
        with jax.named_scope("inverse"):
            gram = mm_high(projected, projected, ((1,), (1,)))
            inverse = inverse_lower(gram)
            new_left = mm_high(inverse, projected)
            if last:
                rows_f32[...] = new_left.T
                left_out[...] = rows_f32[pl.ds(pl.multiple_of(h * OWN, OWN), OWN), :]
            else:
                ls[t] = new_left
        if not last:

            @pl.when(has_below)
            def _():
                send(ls.at[t], lz.at[t], l_send.at[t], l_recv.at[t], (s - 1, h))

        with jax.named_scope("z_cot"):
            mix = mm_high(projected, l_f32[...], ((1,), (1,)))
            z_cot = mm_high(mix, r_f32[:, pl.ds(pl.multiple_of(g1 * LANES, LANES), LANES)])
        drain(zbuf1.at[t, pl.ds(0, NX * NC - 1)], z1_recv.at[t], "z1_recv")
        z_sum = zbuf1[t, 0]
        for j in range(1, NX * NC):
            z_sum = z_sum + zbuf1[t, j]
        zs1[t] = z_sum
        for o in far:
            send(
                zs1.at[t],
                zbuf2.at[t, y],
                z2_send.at[t],
                z2_recv.at[t],
                (s, hid(x, ys[o], c)),
            )
        zbuf2[t, y] = z_sum
        if not last:
            share_rows(t + 1)
            make_mask(t + 1)
        else:
            scatter_merged(chips[10:])
            with jax.named_scope("cot_rows"):
                rows_f32[...] = l_f32[...].T
                own_left = rows_f32[pl.ds(pl.multiple_of(h * OWN, OWN), OWN), :]
                merged = mm_high(own_left, r_f32[...])
        drain(zbuf2.at[t, pl.ds(0, NY - 1)], z2_recv.at[t], "z2_recv")
        with jax.named_scope("r_piece"):
            z_piece = z_cot
            for j in range(NY):
                z_piece = z_piece + zbuf2[t, j]
            r_piece = mm_high(inverse, z_piece)
            rp[t] = r_piece
        if not last:

            @pl.when(has_below)
            def _():
                for i in (2, 1, 3, 0):
                    for e in range(NC):
                        send(
                            rp.at[t],
                            rzbuf.at[t, g1],
                            rz_send.at[t],
                            rz_recv.at[t],
                            (s - 1, hid(xs[i], y, cs[e])),
                        )

        for o, e in group:
            send(
                rp.at[t],
                rbuf.at[t, g1],
                r_send.at[t],
                r_recv.at[t],
                (s, hid(xs[o], y, cs[e])),
            )
        rbuf[t, g1] = r_piece

    t = TICKS - 1
    drain(mbuf.at[pl.ds(0, CHIPS - 1)], m_recv.at[1], "m_recv")
    for k in range(CHIPS):
        merged = merged + mbuf[k].astype(F32)
    grads_out[...] = merged
    drain(rbuf.at[t, pl.ds(0, NX * NC - 1)], r_recv.at[t], "r_recv")
    for j in range(PIECES):
        right_out[:, j * LANES : (j + 1) * LANES] = rbuf[t, j]

    drain(msend.at[0], m_send.at[0])
    drain(mbuf.at[pl.ds(0, CHIPS - 1)], m_send.at[1])
    for t in range(TICKS):
        drain(x_full.at[t, pl.ds(0, CHIPS - 1), 0], ag_send.at[t])
        drain(x_full.at[t, :, 0], agp_send.at[t])
        drain(pbuf1.at[t, pl.ds(0, NX * NC - 1)], p1_send.at[t])
        drain(pbuf2.at[t, pl.ds(0, NY * NC - 1)], p2_send.at[t])
        drain(zbuf1.at[t, pl.ds(0, NX * NC - 1)], z1_send.at[t])
        drain(zbuf2.at[t, pl.ds(0, NY - 1)], z2_send.at[t])
        drain(rbuf.at[t, pl.ds(0, NX * NC - 1)], r_send.at[t])
        if t + 1 < TICKS:

            @pl.when(has_below)
            def _():
                drain(rzbuf.at[t], rz_send.at[t])
                drain(lz.at[t], l_send.at[t])


def hand_over(merged_in, left_in, right_in, merged_out, left_out, right_out):
    merged_out[...] = merged_in[...]
    left_out[...] = left_in[...]
    right_out[...] = right_in[...]


def body(
    section_inputs,
    w_in,
    w_out,
    warm_factor,
    pending_left,
    pending_right,
    incoming_left,
    incoming_right,
):
    width = w_in.shape[2]
    group = NX * NC
    dma = pltpu.SemaphoreType.DMA
    anywhere = pl.BlockSpec(memory_space=pltpu.MemorySpace.HBM)
    inside = pl.BlockSpec(memory_space=pltpu.VMEM)
    results = (
        jax.ShapeDtypeStruct((OWN, D), F32),
        jax.ShapeDtypeStruct((OWN, RANK), F32),
        jax.ShapeDtypeStruct((RANK, D), F32),
    )
    found = pl.pallas_call(
        kernel,
        out_shape=results,
        in_specs=[anywhere] * 8,
        out_specs=(inside, inside, inside),
        scratch_shapes=[
            pltpu.VMEM((D, width), BF16),
            pltpu.VMEM((width, D), BF16),
            pltpu.VMEM((TICKS, CHIPS, NC, OWN, D), BF16),
            pltpu.VMEM((ROWS, width), BF16),
            pltpu.VMEM((ROWS, width), BF16),
            pltpu.VMEM((RANK, ROWS), F32),
            pltpu.VMEM((RANK, D), F32),
            pltpu.VMEM((RANK, D), F32),
            pltpu.VMEM((TICKS, RANK, ROWS), F32),
            pltpu.VMEM((TICKS, RANK, D), F32),
            pltpu.VMEM((TICKS, NC, RANK, LANES), F32),
            pltpu.VMEM((TICKS, group, RANK, LANES), F32),
            pltpu.VMEM((TICKS, RANK, LANES), F32),
            pltpu.VMEM((TICKS, NC * NY, RANK, LANES), F32),
            pltpu.VMEM((TICKS, PIECES, RANK, LANES), F32),
            pltpu.VMEM((TICKS, group, RANK, LANES), F32),
            pltpu.VMEM((TICKS, RANK, LANES), F32),
            pltpu.VMEM((TICKS, NY, RANK, LANES), F32),
            pltpu.VMEM((TICKS, RANK, LANES), F32),
            pltpu.VMEM((TICKS, group, RANK, LANES), F32),
            pltpu.VMEM((TICKS, group, RANK, LANES), F32),
            pltpu.VMEM((TICKS, RANK, ROWS), F32),
            pltpu.VMEM((TICKS, RANK, ROWS), F32),
            pltpu.VMEM((ROWS, RANK), F32),
            pltpu.VMEM((ROWS, D), F32),
            pltpu.VMEM((NC, CHIPS, OWN, D), BF16),
            pltpu.VMEM((CHIPS, OWN, D), BF16),
            pltpu.VMEM((CHIPS, OWN, D), BF16),
            pltpu.VMEM((CHIPS, OWN, D), BF16),
            dma((7,)),
        ]
        + [dma((TICKS,)), dma((TICKS, NX))]
        + [dma((TICKS,))] * 16
        + [dma((2,))] * 2,
        compiler_params=pltpu.CompilerParams(
            collective_id=0, has_side_effects=True, vmem_limit_bytes=67043328
        ),
    )(
        section_inputs[0],
        w_in[0],
        w_out[0],
        jnp.swapaxes(warm_factor[0], 0, 1),
        jnp.swapaxes(pending_left[0], 0, 1),
        jnp.swapaxes(pending_right[0], 0, 1),
        jnp.swapaxes(incoming_left, 1, 2),
        jnp.swapaxes(incoming_right, 1, 2),
    )
    merged, left, right = pl.pallas_call(
        hand_over, out_shape=results, in_specs=[inside] * 3, out_specs=(inside,) * 3
    )(*found)
    return (merged[None], left[None], jnp.swapaxes(right, 0, 1)[None])


def solution(mesh):
    placed = (
        P("pipe", None, "hid", None),
        P("pipe", None, "hid"),
        P("pipe", "hid", None),
        P("pipe", None, None),
        P("pipe", None, None),
        P("pipe", None, None),
        P(),
        P(),
    )
    return jax.shard_map(
        body,
        mesh=mesh,
        in_specs=placed,
        out_specs=(P("pipe", "hid", None), P("pipe", "hid", None), P("pipe", None, None)),
        check_vma=False,
    )
```

```python
import jax
import jax.numpy as jnp
from jax import lax
from jax.experimental import pallas as pl
from jax.experimental.pallas import tpu as pltpu
from jax.sharding import PartitionSpec as P

MESH = pl.DeviceIdType.MESH
F32 = jnp.float32
BF16 = jnp.bfloat16
TICKS = 3
NX, NY, NC = 4, 4, 2
CHIPS = NX * NY
RANK = 16
ROWS = 256
D = 1024
LANES = 128
PIECES = D // LANES
OWN = ROWS // (CHIPS * NC)
HALF = RANK // 2
GROUP = NX * NC


def split(value):
    high = value.astype(BF16)
    low = (value - high.astype(F32)).astype(BF16)
    return high, low


def mm(first, second, dims=((1,), (0,))):
    return lax.dot_general(first, second, (dims, ((), ())), preferred_element_type=F32)


def mm_high(first, second, dims=((1,), (0,))):
    return lax.dot_general(
        first,
        second,
        (dims, ((), ())),
        precision=lax.Precision.HIGHEST,
        preferred_element_type=F32,
    )


def thin(value, matrix, dims):
    high, low = split(value)
    both = mm(jnp.concatenate([high, low], axis=0), matrix, dims)
    return both[:RANK] + both[RANK:]


def times(inverse, value):
    first_high, first_low = split(inverse)
    high, low = split(value)
    return mm(
        jnp.concatenate([first_high, first_high, first_low], axis=1),
        jnp.concatenate([high, low, high], axis=0),
    )


def inverse_lower(gram):
    row = lax.broadcasted_iota(jnp.int32, (RANK, LANES), 0)
    lane = lax.broadcasted_iota(jnp.int32, (RANK, LANES), 1)
    work = jnp.concatenate([gram, jnp.zeros((RANK, LANES - RANK), F32)], axis=1)
    work = work + jnp.where(lane == row + RANK, 1.0, 0.0).astype(F32)
    pivots = jnp.zeros((RANK, LANES), F32)
    for k in range(RANK):
        column = jnp.broadcast_to(work[:, k : k + 1], (RANK, LANES))
        pivot = jnp.broadcast_to(column[k : k + 1, :], (RANK, LANES))
        along = jnp.broadcast_to(work[k : k + 1, :], (RANK, LANES))
        factor = jnp.where(row > k, column / pivot, 0.0)
        work = work - factor * along
        pivots = jnp.where(row == k, pivot, pivots)
    scaled = work * lax.rsqrt(pivots)
    return scaled[:, RANK : 2 * RANK]


def kernel(
    x_hbm,
    wi_hbm,
    wo_hbm,
    warm_hbm,
    pend_l_hbm,
    pend_r_hbm,
    inc_l_hbm,
    inc_r_hbm,
    grads_out,
    left_out,
    right_out,
    wi,
    wo,
    x_full,
    mask,
    hg,
    l_f32,
    r_f32,
    b_f32,
    l_inc,
    r_inc,
    ps,
    pbuf1,
    ps1,
    pbuf2,
    zs,
    zbuf1,
    zs1,
    zbuf2,
    zc,
    zp,
    z_full,
    a_f32,
    m_high,
    m_low,
    rbuf,
    rzbuf,
    ls,
    lz,
    rows_f32,
    mfull,
    msend,
    mpair,
    mpart,
    mbuf,
    local_sem,
    ag_send,
    ag_recv,
    agp_send,
    agp_recv,
    p1_send,
    p1_recv,
    p2_send,
    p2_recv,
    z1_send,
    z1_recv,
    z2_send,
    z2_recv,
    r_send,
    r_recv,
    rz_send,
    rz_recv,
    l_send,
    l_recv,
    m_send,
    m_recv,
):
    s = lax.axis_index("pipe")
    last_section = lax.axis_size("pipe") - 1
    h = lax.axis_index("hid")
    chip = h // NC
    c = h % NC
    x = chip // NY
    y = chip % NY
    oc = 1 - c
    xs = [x] + [(x + o) % NX for o in range(1, NX)]
    ys = [y] + [(y + o) % NY for o in range(1, NY)]
    cs = [c, oc]
    g1 = x * NC + c
    g2 = y * NC + c
    is_top = s == last_section
    has_above = s < last_section
    has_below = s > 0
    far = (2, 1, 3)
    group = [(o, e) for o in far for e in range(NC)] + [(0, 1)]
    chips = [(i, j) for i in (2, 1, 3, 0) for j in (2, 1, 3, 0) if (i, j) != (0, 0)]

    def hid(xx, yy, cc):
        return xx * (NY * NC) + yy * NC + cc

    def send(src, dst, send_sem, recv_sem, target):
        pltpu.make_async_remote_copy(
            src_ref=src,
            dst_ref=dst,
            send_sem=send_sem,
            recv_sem=recv_sem,
            device_id=target,
            device_id_type=MESH,
        ).start()

    def drain(ref, sem, name="out"):
        with jax.named_scope(name):
            pltpu.make_async_copy(ref, ref, sem).wait()

    barrier = pltpu.get_barrier_semaphore()

    def signal(target):
        pl.semaphore_signal(barrier, inc=1, device_id=target, device_id_type=MESH)

    for i, j in chips:
        signal((s, hid(xs[i], ys[j], c)))

    @pl.when(has_below)
    def _():
        for e in range(NC):
            for i in range(NX):
                signal((s - 1, hid(xs[i], y, cs[e])))
            for i in far:
                signal((s - 1, hid(x, ys[i], cs[e])))

    @pl.when(has_above)
    def _():
        for e in range(NC):
            for i in range(NX):
                signal((s + 1, hid(xs[i], y, cs[e])))
            for i in far:
                signal((s + 1, hid(x, ys[i], cs[e])))

    for o in far:
        signal((s, hid(xs[o], y, oc)))
        signal((s, hid(x, ys[o], oc)))
    signal((s, hid(x, y, oc)))

    own_x = [
        pltpu.make_async_copy(x_hbm.at[t], x_full.at[t, chip, c], ag_recv.at[t, 0])
        for t in range(TICKS)
    ]
    for copy in own_x:
        copy.start()
    loads = [
        pltpu.make_async_copy(warm_hbm, b_f32, local_sem.at[0]),
        pltpu.make_async_copy(inc_l_hbm, l_inc, local_sem.at[3]),
        pltpu.make_async_copy(inc_r_hbm, r_inc, local_sem.at[4]),
        pltpu.make_async_copy(pend_l_hbm, l_f32, local_sem.at[5]),
        pltpu.make_async_copy(pend_r_hbm, r_f32, local_sem.at[6]),
        pltpu.make_async_copy(wo_hbm, wo, local_sem.at[1]),
        pltpu.make_async_copy(wi_hbm, wi, local_sem.at[2]),
    ]
    for load in loads:
        load.start()

    neighbours = has_below.astype(jnp.int32) + has_above.astype(jnp.int32)
    with jax.named_scope("entry"):
        pl.semaphore_wait(barrier, CHIPS + 2 * (NX - 1) + NC * (NX + NY - 1) * neighbours)

    def gather_rows(t, targets):
        for i, j in targets:
            send(
                x_hbm.at[t],
                x_full.at[t, chip, c],
                ag_send.at[t],
                ag_recv.at[t, (NX - i) % NX],
                (s, hid(xs[i], ys[j], c)),
            )

    def share_rows(t):
        for i in (0, 1, 3, 2):
            four = x_full.at[t, pl.ds(xs[i] * NY, NY), c]
            drain(four, ag_recv.at[t, i], "ag_recv")
            send(four, four, agp_send.at[t], agp_recv.at[t], (s, hid(x, y, oc)))

    def make_mask(t):
        drain(x_full.at[t, :, oc], agp_recv.at[t], "agp_recv")
        with jax.named_scope("mask"):
            rows = x_full[t].reshape(ROWS, D)
            preact = mm(rows, wi[...])
            mask[...] = jnp.where(preact > 0, 1.0, 0.0).astype(BF16)

    def scatter_merged(targets):
        for i, j in targets:
            send(
                mpart.at[xs[i] * NY + ys[j]],
                mbuf.at[chip],
                m_send.at[1],
                m_recv.at[1],
                (s, hid(xs[i], ys[j], c)),
            )

    def unpack(pieces, t):
        for j in range(PIECES):
            for e in range(NC):
                z_full[e * HALF : (e + 1) * HALF, j * LANES : (j + 1) * LANES] = pieces[t, j * NC + e]
        return z_full[...]

    def total(pieces, t, base, count):
        value = pieces[t, base]
        for j in range(1, count):
            value = value + pieces[t, base + j]
        return value

    def three_columns():
        high, low = split(a_f32[...])
        return jnp.concatenate([high, high, low], axis=0).T

    def low_cotangent(columns):
        high, low = split(z_full[...])
        return mm(columns, jnp.concatenate([high, low, high], axis=0)).astype(BF16)

    gather_rows(0, chips)
    with jax.named_scope("loads"):
        for load in loads:
            load.wait()

    @pl.when(is_top)
    def _():
        l_f32[...] = l_inc[0]
        r_f32[...] = r_inc[0]

    a_f32[...] = l_f32[...]
    z_full[...] = r_f32[...]
    for t in range(TICKS):
        last = t + 1 == TICKS
        if t > 0:
            drain(rbuf.at[t - 1, pl.ds(0, 2 * (GROUP - 1))], r_recv.at[t - 1], "r_recv")
            b_f32[...] = times(inverse, unpack(rbuf, t - 1))
        with jax.named_scope("v"):
            v = thin(b_f32[...], wi[...], ((1,), (0,)))
        if t > 0:

            @pl.when(has_above)
            def _():
                drain(lz.at[t - 1], l_recv.at[t - 1], "l_recv")
                l_f32[...] = lz[t - 1, :, :ROWS]
                above = lz[t - 1, :, ROWS : ROWS + RANK]
                a_f32[...] = mm_high(above, l_f32[...], ((0,), (0,)))

            @pl.when(is_top)
            def _():
                l_f32[...] = l_inc[t]
                a_f32[...] = l_inc[t]
                z_full[...] = r_inc[t]

        columns = three_columns()
        if t > 0:

            @pl.when(has_above)
            def _():
                drain(rzbuf.at[t - 1], rz_recv.at[t - 1], "rz_recv")
                unpack(rzbuf, t - 1)

        with jax.named_scope("upward"):
            upward = mm(low_cotangent(columns), wo[...], ((1,), (1,)))
            if t > 0:
                hg[...] = upward.astype(BF16) * mask[...]
            else:
                hg[...] = upward.astype(BF16)
        if t == 0:
            share_rows(0)
            make_mask(0)
            hg[...] = hg[...] * mask[...]
        with jax.named_scope("p_part"):
            p_part = thin(v, hg[...], ((1,), (1,)))
            for e in range(NC):
                for k in range(2):
                    ps[t, e, k] = p_part[k * HALF : (k + 1) * HALF, e * LANES : (e + 1) * LANES]
        for o, e in group:
            send(
                ps.at[t, cs[e], 0],
                pbuf1.at[t, g1],
                p1_send.at[t],
                p1_recv.at[t],
                (s, hid(xs[o], y, cs[e])),
            )
            send(
                ps.at[t, cs[e], 1],
                pbuf1.at[t, GROUP + g2],
                p1_send.at[t],
                p1_recv.at[t],
                (s, hid(x, ys[o], cs[e])),
            )
        pbuf1[t, g1] = ps[t, c, 0]
        pbuf1[t, GROUP + g2] = ps[t, c, 1]
        if not last:
            gather_rows(t + 1, chips[:5])
        if t > 0:

            @pl.when(has_above)
            def _():
                above = lz[t - 1, :, ROWS : ROWS + RANK]
                r_f32[...] = times(above, z_full[...])

            @pl.when(is_top)
            def _():
                r_f32[...] = z_full[...]

        with jax.named_scope("p_cot"):
            cross = mm_high(b_f32[...], r_f32[...], ((1,), (1,)))
            p_cot = mm_high(cross, l_f32[...])
        with jax.named_scope("merged"):
            partial = mm(hg[...], wi[...], ((1,), (1,)))
            if last:
                mfull[...] = partial
            partial_high, partial_low = split(partial)
            m_high[...] = partial_high
            m_low[...] = partial_low
        if last:
            for k in range(CHIPS):
                for e in range(NC):
                    base = (k * NC + e) * OWN
                    msend[e, k] = mfull[base : base + OWN, :].astype(BF16)
            send(
                msend.at[oc],
                mpair,
                m_send.at[0],
                m_recv.at[0],
                (s, hid(x, y, oc)),
            )
        drain(pbuf1.at[t, pl.ds(0, 2 * (GROUP - 1))], p1_recv.at[t], "p1_recv")
        first = total(pbuf1, t, 0, GROUP)
        second = total(pbuf1, t, GROUP, GROUP)
        ps1[t, 0] = first
        ps1[t, 1] = second
        for o, e in group:
            send(
                ps1.at[t, 0],
                pbuf2.at[t, c * NY + y],
                p2_send.at[t],
                p2_recv.at[t],
                (s, hid(x, ys[o], cs[e])),
            )
            send(
                ps1.at[t, 1],
                pbuf2.at[t, GROUP + c * NX + x],
                p2_send.at[t],
                p2_recv.at[t],
                (s, hid(xs[o], y, cs[e])),
            )
        pbuf2[t, c * NY + y] = first
        pbuf2[t, GROUP + c * NX + x] = second
        if last:
            drain(mpair, m_recv.at[0], "m_recv")
            with jax.named_scope("mpart"):
                mpart[...] = (msend[c].astype(F32) + mpair[...].astype(F32)).astype(BF16)
            scatter_merged(chips[:5])
            mbuf[chip] = mpart[chip]
        else:
            gather_rows(t + 1, chips[5:10])
        drain(pbuf2.at[t, pl.ds(0, 2 * (GROUP - 1))], p2_recv.at[t], "p2_recv")
        with jax.named_scope("z_part"):
            halves = []
            for k in range(2):
                two = [total(pbuf2, t, k * GROUP + e * NY, NY) for e in range(NC)]
                halves.append(jnp.concatenate(two, axis=1))
            projected = jnp.concatenate(halves, axis=0) + p_cot
            z_part = thin(projected, m_high[...], ((1,), (0,)))
            z_part = z_part + mm(projected.astype(BF16), m_low[...])
            for j in range(PIECES):
                for e in range(NC):
                    zs[t, j * NC + e] = z_part[e * HALF : (e + 1) * HALF, j * LANES : (j + 1) * LANES]
        for o, e in group:
            send(
                zs.at[t, xs[o] * NC + cs[e]],
                zbuf1.at[t, g1],
                z1_send.at[t],
                z1_recv.at[t],
                (s, hid(xs[o], y, cs[e])),
            )
            send(
                zs.at[t, GROUP + ys[o] * NC + cs[e]],
                zbuf1.at[t, GROUP + g2],
                z1_send.at[t],
                z1_recv.at[t],
                (s, hid(x, ys[o], cs[e])),
            )
        zbuf1[t, g1] = zs[t, g1]
        zbuf1[t, GROUP + g2] = zs[t, GROUP + g2]
        if last:
            scatter_merged(chips[5:10])
        else:
            gather_rows(t + 1, chips[10:])
        with jax.named_scope("inverse"):
            gram = mm_high(projected, projected, ((1,), (1,)))
            inverse = inverse_lower(gram)
            new_left = mm_high(inverse, projected)
            if last:
                rows_f32[...] = new_left.T
                left_out[...] = rows_f32[pl.ds(pl.multiple_of(h * OWN, OWN), OWN), :]
            else:
                ls[t, :, :ROWS] = new_left
                ls[t, :, ROWS:] = jnp.concatenate([inverse, jnp.zeros((RANK, LANES - RANK), F32)], axis=1)
        if not last:

            @pl.when(has_below)
            def _():
                send(ls.at[t], lz.at[t], l_send.at[t], l_recv.at[t], (s - 1, h))

        with jax.named_scope("z_cot"):
            mix = mm_high(projected, l_f32[...], ((1,), (1,)))
            for k, place in enumerate((x, NX + y)):
                lanes = pl.ds(pl.multiple_of(place * LANES, LANES), LANES)
                z_cot = mm_high(mix, r_f32[:, lanes])
                for e in range(NC):
                    zc[k, e] = z_cot[e * HALF : (e + 1) * HALF, :]
        drain(zbuf1.at[t, pl.ds(0, 2 * (GROUP - 1))], z1_recv.at[t], "z1_recv")
        first = total(zbuf1, t, 0, GROUP)
        second = total(zbuf1, t, GROUP, GROUP)
        zs1[t, 0] = first
        zs1[t, 1] = second
        for o in far:
            send(
                zs1.at[t, 0],
                zbuf2.at[t, y],
                z2_send.at[t],
                z2_recv.at[t],
                (s, hid(x, ys[o], c)),
            )
            send(
                zs1.at[t, 1],
                zbuf2.at[t, NY + x],
                z2_send.at[t],
                z2_recv.at[t],
                (s, hid(xs[o], y, c)),
            )
        zbuf2[t, y] = first
        zbuf2[t, NY + x] = second
        if not last:
            share_rows(t + 1)
            make_mask(t + 1)
        else:
            scatter_merged(chips[10:])
            with jax.named_scope("cot_rows"):
                rows_f32[...] = l_f32[...].T
                own_left = rows_f32[pl.ds(pl.multiple_of(h * OWN, OWN), OWN), :]
                merged = mm_high(own_left, r_f32[...])
        drain(zbuf2.at[t, pl.ds(0, 2 * (NY - 1))], z2_recv.at[t], "z2_recv")
        with jax.named_scope("r_piece"):
            first = total(zbuf2, t, 0, NY) + zc[0, c]
            second = total(zbuf2, t, NY, NX) + zc[1, c]
            zp[t, 0] = first
            zp[t, 1] = second
        slots = (g1, GROUP + g2)
        if not last:

            @pl.when(has_below)
            def _():
                for i in (2, 1, 3, 0):
                    for e in range(NC):
                        for k, place in enumerate((hid(xs[i], y, cs[e]), hid(x, ys[i], cs[e]))):
                            send(
                                zp.at[t, k],
                                rzbuf.at[t, slots[k]],
                                rz_send.at[t],
                                rz_recv.at[t],
                                (s - 1, place),
                            )

        for o, e in group:
            for k, place in enumerate((hid(xs[o], y, cs[e]), hid(x, ys[o], cs[e]))):
                send(
                    zp.at[t, k],
                    rbuf.at[t, slots[k]],
                    r_send.at[t],
                    r_recv.at[t],
                    (s, place),
                )
        rbuf[t, g1] = first
        rbuf[t, GROUP + g2] = second

    t = TICKS - 1
    drain(mbuf.at[pl.ds(0, CHIPS - 1)], m_recv.at[1], "m_recv")
    for k in range(CHIPS):
        merged = merged + mbuf[k].astype(F32)
    grads_out[...] = merged
    drain(rbuf.at[t, pl.ds(0, 2 * (GROUP - 1))], r_recv.at[t], "r_recv")
    right_out[...] = times(inverse, unpack(rbuf, t))

    drain(msend.at[0], m_send.at[0])
    drain(mbuf.at[pl.ds(0, CHIPS - 1)], m_send.at[1])
    for t in range(TICKS):
        drain(x_full.at[t, pl.ds(0, CHIPS - 1), 0], ag_send.at[t])
        drain(x_full.at[t, :, 0], agp_send.at[t])
        drain(pbuf1.at[t, pl.ds(0, 2 * (GROUP - 1))], p1_send.at[t])
        drain(pbuf2.at[t, pl.ds(0, 2 * (GROUP - 1))], p2_send.at[t])
        drain(zbuf1.at[t, pl.ds(0, 2 * (GROUP - 1))], z1_send.at[t])
        drain(zbuf2.at[t, pl.ds(0, 2 * (NY - 1))], z2_send.at[t])
        drain(rbuf.at[t, pl.ds(0, 2 * (GROUP - 1))], r_send.at[t])
        if t + 1 < TICKS:

            @pl.when(has_below)
            def _():
                drain(rzbuf.at[t], rz_send.at[t])
                drain(lz.at[t], l_send.at[t])


def hand_over(merged_in, left_in, right_in, merged_out, left_out, right_out):
    merged_out[...] = merged_in[...]
    left_out[...] = left_in[...]
    right_out[...] = right_in[...]


def body(
    section_inputs,
    w_in,
    w_out,
    warm_factor,
    pending_left,
    pending_right,
    incoming_left,
    incoming_right,
):
    width = w_in.shape[2]
    dma = pltpu.SemaphoreType.DMA
    anywhere = pl.BlockSpec(memory_space=pltpu.MemorySpace.HBM)
    inside = pl.BlockSpec(memory_space=pltpu.VMEM)
    results = (
        jax.ShapeDtypeStruct((OWN, D), F32),
        jax.ShapeDtypeStruct((OWN, RANK), F32),
        jax.ShapeDtypeStruct((RANK, D), F32),
    )
    found = pl.pallas_call(
        kernel,
        out_shape=results,
        in_specs=[anywhere] * 8,
        out_specs=(inside, inside, inside),
        scratch_shapes=[
            pltpu.VMEM((D, width), BF16),
            pltpu.VMEM((width, D), BF16),
            pltpu.VMEM((TICKS, CHIPS, NC, OWN, D), BF16),
            pltpu.VMEM((ROWS, width), BF16),
            pltpu.VMEM((ROWS, width), BF16),
            pltpu.VMEM((RANK, ROWS), F32),
            pltpu.VMEM((RANK, D), F32),
            pltpu.VMEM((RANK, D), F32),
            pltpu.VMEM((TICKS, RANK, ROWS), F32),
            pltpu.VMEM((TICKS, RANK, D), F32),
            pltpu.VMEM((TICKS, NC, 2, HALF, LANES), F32),
            pltpu.VMEM((TICKS, 2 * GROUP, HALF, LANES), F32),
            pltpu.VMEM((TICKS, 2, HALF, LANES), F32),
            pltpu.VMEM((TICKS, 2 * GROUP, HALF, LANES), F32),
            pltpu.VMEM((TICKS, 2 * GROUP, HALF, LANES), F32),
            pltpu.VMEM((TICKS, 2 * GROUP, HALF, LANES), F32),
            pltpu.VMEM((TICKS, 2, HALF, LANES), F32),
            pltpu.VMEM((TICKS, NY + NX, HALF, LANES), F32),
            pltpu.VMEM((2, NC, HALF, LANES), F32),
            pltpu.VMEM((TICKS, 2, HALF, LANES), F32),
            pltpu.VMEM((RANK, D), F32),
            pltpu.VMEM((RANK, ROWS), F32),
            pltpu.VMEM((ROWS, D), BF16),
            pltpu.VMEM((ROWS, D), BF16),
            pltpu.VMEM((TICKS, 2 * GROUP, HALF, LANES), F32),
            pltpu.VMEM((TICKS, 2 * GROUP, HALF, LANES), F32),
            pltpu.VMEM((TICKS, RANK, ROWS + LANES), F32),
            pltpu.VMEM((TICKS, RANK, ROWS + LANES), F32),
            pltpu.VMEM((ROWS, RANK), F32),
            pltpu.VMEM((ROWS, D), F32),
            pltpu.VMEM((NC, CHIPS, OWN, D), BF16),
            pltpu.VMEM((CHIPS, OWN, D), BF16),
            pltpu.VMEM((CHIPS, OWN, D), BF16),
            pltpu.VMEM((CHIPS, OWN, D), BF16),
            dma((7,)),
        ]
        + [dma((TICKS,)), dma((TICKS, NX))]
        + [dma((TICKS,))] * 16
        + [dma((2,))] * 2,
        compiler_params=pltpu.CompilerParams(
            collective_id=0, has_side_effects=True, vmem_limit_bytes=67043328
        ),
    )(
        section_inputs[0],
        w_in[0],
        w_out[0],
        jnp.swapaxes(warm_factor[0], 0, 1),
        jnp.swapaxes(pending_left[0], 0, 1),
        jnp.swapaxes(pending_right[0], 0, 1),
        jnp.swapaxes(incoming_left, 1, 2),
        jnp.swapaxes(incoming_right, 1, 2),
    )
    merged, left, right = pl.pallas_call(
        hand_over, out_shape=results, in_specs=[inside] * 3, out_specs=(inside,) * 3
    )(*found)
    return (merged[None], left[None], jnp.swapaxes(right, 0, 1)[None])


def solution(mesh):
    placed = (
        P("pipe", None, "hid", None),
        P("pipe", None, "hid"),
        P("pipe", "hid", None),
        P("pipe", None, None),
        P("pipe", None, None),
        P("pipe", None, None),
        P(),
        P(),
    )
    return jax.shard_map(
        body,
        mesh=mesh,
        in_specs=placed,
        out_specs=(P("pipe", "hid", None), P("pipe", "hid", None), P("pipe", None, None)),
        check_vma=False,
    )
```

```python
import jax
import jax.numpy as jnp
from jax import lax
from jax.experimental import pallas as pl
from jax.experimental.pallas import tpu as pltpu
from jax.sharding import PartitionSpec as P

MESH = pl.DeviceIdType.MESH
F32 = jnp.float32
BF16 = jnp.bfloat16
TICKS = 3
NX, NY, NC = 4, 4, 2
CHIPS = NX * NY
RANK = 16
ROWS = 256
D = 1024
LANES = 128
PIECES = D // LANES
OWN = ROWS // (CHIPS * NC)
HALF = RANK // 2
GROUP = NX * NC


def split(value):
    high = value.astype(BF16)
    low = (value - high.astype(F32)).astype(BF16)
    return high, low


def mm(first, second, dims=((1,), (0,))):
    return lax.dot_general(first, second, (dims, ((), ())), preferred_element_type=F32)


def mm_high(first, second, dims=((1,), (0,))):
    return lax.dot_general(
        first,
        second,
        (dims, ((), ())),
        precision=lax.Precision.HIGHEST,
        preferred_element_type=F32,
    )


def thin(value, matrix, dims):
    high, low = split(value)
    both = mm(jnp.concatenate([high, low], axis=0), matrix, dims)
    return both[:RANK] + both[RANK:]


def times(inverse, value):
    first_high, first_low = split(inverse)
    high, low = split(value)
    return mm(
        jnp.concatenate([first_high, first_high, first_low], axis=1),
        jnp.concatenate([high, low, high], axis=0),
    )


def inverse_lower(gram):
    row = lax.broadcasted_iota(jnp.int32, (RANK, LANES), 0)
    lane = lax.broadcasted_iota(jnp.int32, (RANK, LANES), 1)
    work = jnp.concatenate([gram, jnp.zeros((RANK, LANES - RANK), F32)], axis=1)
    work = work + jnp.where(lane == row + RANK, 1.0, 0.0).astype(F32)
    pivots = jnp.zeros((RANK, LANES), F32)
    for k in range(RANK):
        column = jnp.broadcast_to(work[:, k : k + 1], (RANK, LANES))
        pivot = jnp.broadcast_to(column[k : k + 1, :], (RANK, LANES))
        along = jnp.broadcast_to(work[k : k + 1, :], (RANK, LANES))
        factor = jnp.where(row > k, column / pivot, 0.0)
        work = work - factor * along
        pivots = jnp.where(row == k, pivot, pivots)
    scaled = work * lax.rsqrt(pivots)
    return scaled[:, RANK : 2 * RANK]


def kernel(
    x_hbm,
    wi_hbm,
    wo_hbm,
    warm_hbm,
    pend_l_hbm,
    pend_r_hbm,
    inc_l_hbm,
    inc_r_hbm,
    grads_out,
    left_out,
    right_out,
    wi,
    wo,
    x_full,
    mask,
    hg,
    l_f32,
    r_f32,
    b_f32,
    l_inc,
    r_inc,
    ps,
    pbuf1,
    ps1,
    pbuf2,
    zs,
    zbuf1,
    zs1,
    zbuf2,
    zc,
    zp,
    z_full,
    a_f32,
    m_high,
    m_low,
    rbuf,
    rzbuf,
    ls,
    lz,
    rows_f32,
    mfull,
    msend,
    mpair,
    mpart,
    mbuf,
    local_sem,
    ag_send,
    ag_recv,
    agp_send,
    agp_recv,
    p1_send,
    p1_recv,
    p2_send,
    p2_recv,
    z1_send,
    z1_recv,
    z2_send,
    z2_recv,
    r_send,
    r_recv,
    rz_send,
    rz_recv,
    l_send,
    l_recv,
    m_send,
    m_recv,
):
    s = lax.axis_index("pipe")
    last_section = lax.axis_size("pipe") - 1
    h = lax.axis_index("hid")
    chip = h // NC
    c = h % NC
    x = chip // NY
    y = chip % NY
    oc = 1 - c
    xs = [x] + [(x + o) % NX for o in range(1, NX)]
    ys = [y] + [(y + o) % NY for o in range(1, NY)]
    cs = [c, oc]
    g1 = x * NC + c
    g2 = y * NC + c
    is_top = s == last_section
    has_above = s < last_section
    has_below = s > 0
    far = (2, 1, 3)
    group = [(o, e) for o in far for e in range(NC)] + [(0, 1)]
    chips = [(i, j) for i in (2, 1, 3, 0) for j in (2, 1, 3, 0) if (i, j) != (0, 0)]

    def hid(xx, yy, cc):
        return xx * (NY * NC) + yy * NC + cc

    def send(src, dst, send_sem, recv_sem, target):
        pltpu.make_async_remote_copy(
            src_ref=src,
            dst_ref=dst,
            send_sem=send_sem,
            recv_sem=recv_sem,
            device_id=target,
            device_id_type=MESH,
        ).start()

    def drain(ref, sem, name="out"):
        with jax.named_scope(name):
            pltpu.make_async_copy(ref, ref, sem).wait()

    barrier = pltpu.get_barrier_semaphore()

    def signal(target):
        pl.semaphore_signal(barrier, inc=1, device_id=target, device_id_type=MESH)

    for i, j in chips:
        signal((s, hid(xs[i], ys[j], c)))

    @pl.when(has_below)
    def _():
        for e in range(NC):
            for i in range(NX):
                signal((s - 1, hid(xs[i], y, cs[e])))
            for i in far:
                signal((s - 1, hid(x, ys[i], cs[e])))

    @pl.when(has_above)
    def _():
        for e in range(NC):
            for i in range(NX):
                signal((s + 1, hid(xs[i], y, cs[e])))
            for i in far:
                signal((s + 1, hid(x, ys[i], cs[e])))

    for o in far:
        signal((s, hid(xs[o], y, oc)))
        signal((s, hid(x, ys[o], oc)))
    signal((s, hid(x, y, oc)))

    own_x = [
        pltpu.make_async_copy(x_hbm.at[t], x_full.at[t, chip, c], ag_recv.at[t, 0])
        for t in range(TICKS)
    ]
    for copy in own_x:
        copy.start()
    loads = [
        pltpu.make_async_copy(warm_hbm, b_f32, local_sem.at[0]),
        pltpu.make_async_copy(inc_l_hbm, l_inc, local_sem.at[3]),
        pltpu.make_async_copy(inc_r_hbm, r_inc, local_sem.at[4]),
        pltpu.make_async_copy(pend_l_hbm, l_f32, local_sem.at[5]),
        pltpu.make_async_copy(pend_r_hbm, r_f32, local_sem.at[6]),
        pltpu.make_async_copy(wo_hbm, wo, local_sem.at[1]),
        pltpu.make_async_copy(wi_hbm, wi, local_sem.at[2]),
    ]
    for load in loads:
        load.start()

    neighbours = has_below.astype(jnp.int32) + has_above.astype(jnp.int32)
    with jax.named_scope("entry"):
        pl.semaphore_wait(barrier, CHIPS + 2 * (NX - 1) + NC * (NX + NY - 1) * neighbours)

    def gather_rows(t, targets):
        for i, j in targets:
            send(
                x_hbm.at[t],
                x_full.at[t, chip, c],
                ag_send.at[t],
                ag_recv.at[t, (NX - i) % NX],
                (s, hid(xs[i], ys[j], c)),
            )

    def share_rows(t):
        for i in (0, 1, 3, 2):
            four = x_full.at[t, pl.ds(xs[i] * NY, NY), c]
            drain(four, ag_recv.at[t, i], "ag_recv")
            send(four, four, agp_send.at[t], agp_recv.at[t], (s, hid(x, y, oc)))

    def make_mask(t):
        drain(x_full.at[t, :, oc], agp_recv.at[t], "agp_recv")
        with jax.named_scope("mask"):
            rows = x_full[t].reshape(ROWS, D)
            preact = mm(rows, wi[...])
            mask[...] = jnp.where(preact > 0, 1.0, 0.0).astype(BF16)

    def scatter_merged(targets):
        for i, j in targets:
            send(
                mpart.at[xs[i] * NY + ys[j]],
                mbuf.at[chip],
                m_send.at[1],
                m_recv.at[1],
                (s, hid(xs[i], ys[j], c)),
            )

    def unpack(pieces, t):
        for j in range(PIECES):
            for e in range(NC):
                z_full[e * HALF : (e + 1) * HALF, j * LANES : (j + 1) * LANES] = pieces[t, j * NC + e]
        return z_full[...]

    def total(pieces, t, base, count):
        value = pieces[t, base]
        for j in range(1, count):
            value = value + pieces[t, base + j]
        return value

    def three_columns():
        high, low = split(a_f32[...])
        return jnp.concatenate([high, high, low], axis=0).T

    def low_cotangent(columns):
        high, low = split(z_full[...])
        return mm(columns, jnp.concatenate([high, low, high], axis=0)).astype(BF16)

    gather_rows(0, chips)
    with jax.named_scope("loads"):
        for load in loads:
            load.wait()

    @pl.when(is_top)
    def _():
        l_f32[...] = l_inc[0]
        r_f32[...] = r_inc[0]

    a_f32[...] = l_f32[...]
    z_full[...] = r_f32[...]
    for t in range(TICKS):
        last = t + 1 == TICKS
        if t > 0:
            drain(rbuf.at[t - 1, pl.ds(0, 2 * (GROUP - 1))], r_recv.at[t - 1], "r_recv")
            b_f32[...] = times(inverse, unpack(rbuf, t - 1))
        with jax.named_scope("v"):
            v = thin(b_f32[...], wi[...], ((1,), (0,)))
        if t > 0:

            @pl.when(has_above)
            def _():
                drain(lz.at[t - 1], l_recv.at[t - 1], "l_recv")
                l_f32[...] = lz[t - 1, :, :ROWS]
                above = lz[t - 1, :, ROWS : ROWS + RANK]
                a_f32[...] = mm_high(above, l_f32[...], ((0,), (0,)))

            @pl.when(is_top)
            def _():
                l_f32[...] = l_inc[t]
                a_f32[...] = l_inc[t]
                z_full[...] = r_inc[t]

        columns = three_columns()
        if t > 0:

            @pl.when(has_above)
            def _():
                drain(rzbuf.at[t - 1], rz_recv.at[t - 1], "rz_recv")
                unpack(rzbuf, t - 1)

        with jax.named_scope("upward"):
            upward = mm(low_cotangent(columns), wo[...], ((1,), (1,)))
            if t > 0:
                hg[...] = upward.astype(BF16) * mask[...]
            else:
                hg[...] = upward.astype(BF16)
        if t == 0:
            share_rows(0)
            make_mask(0)
            hg[...] = hg[...] * mask[...]
        with jax.named_scope("p_part"):
            p_part = thin(v, hg[...], ((1,), (1,)))
            for e in range(NC):
                for k in range(2):
                    ps[t, e, k] = p_part[k * HALF : (k + 1) * HALF, e * LANES : (e + 1) * LANES]
        for o, e in group:
            send(
                ps.at[t, cs[e], 0],
                pbuf1.at[t, g1],
                p1_send.at[t],
                p1_recv.at[t],
                (s, hid(xs[o], y, cs[e])),
            )
            send(
                ps.at[t, cs[e], 1],
                pbuf1.at[t, GROUP + g2],
                p1_send.at[t],
                p1_recv.at[t],
                (s, hid(x, ys[o], cs[e])),
            )
        pbuf1[t, g1] = ps[t, c, 0]
        pbuf1[t, GROUP + g2] = ps[t, c, 1]
        if not last:
            gather_rows(t + 1, chips[:5])
        if t > 0:

            @pl.when(has_above)
            def _():
                above = lz[t - 1, :, ROWS : ROWS + RANK]
                r_f32[...] = times(above, z_full[...])

            @pl.when(is_top)
            def _():
                r_f32[...] = z_full[...]

        with jax.named_scope("p_cot"):
            cross = mm_high(b_f32[...], r_f32[...], ((1,), (1,)))
            p_cot = mm_high(cross, l_f32[...])
        with jax.named_scope("merged"):
            partial = mm(hg[...], wi[...], ((1,), (1,)))
            if last:
                mfull[...] = partial
            partial_high, partial_low = split(partial)
            m_high[...] = partial_high
            m_low[...] = partial_low
        if last:
            for k in range(CHIPS):
                for e in range(NC):
                    base = (k * NC + e) * OWN
                    msend[e, k] = mfull[base : base + OWN, :].astype(BF16)
            send(
                msend.at[oc],
                mpair,
                m_send.at[0],
                m_recv.at[0],
                (s, hid(x, y, oc)),
            )
        drain(pbuf1.at[t, pl.ds(0, 2 * (GROUP - 1))], p1_recv.at[t], "p1_recv")
        first = total(pbuf1, t, 0, GROUP)
        second = total(pbuf1, t, GROUP, GROUP)
        ps1[t, 0] = first
        ps1[t, 1] = second
        for o, e in group:
            send(
                ps1.at[t, 0],
                pbuf2.at[t, c * NY + y],
                p2_send.at[t],
                p2_recv.at[t],
                (s, hid(x, ys[o], cs[e])),
            )
            send(
                ps1.at[t, 1],
                pbuf2.at[t, GROUP + c * NX + x],
                p2_send.at[t],
                p2_recv.at[t],
                (s, hid(xs[o], y, cs[e])),
            )
        pbuf2[t, c * NY + y] = first
        pbuf2[t, GROUP + c * NX + x] = second
        if last:
            drain(mpair, m_recv.at[0], "m_recv")
            with jax.named_scope("mpart"):
                mpart[...] = (msend[c].astype(F32) + mpair[...].astype(F32)).astype(BF16)
            scatter_merged(chips[:5])
            mbuf[chip] = mpart[chip]
        else:
            gather_rows(t + 1, chips[5:10])
        drain(pbuf2.at[t, pl.ds(0, 2 * (GROUP - 1))], p2_recv.at[t], "p2_recv")
        with jax.named_scope("z_part"):
            halves = []
            for k in range(2):
                two = [total(pbuf2, t, k * GROUP + e * NY, NY) for e in range(NC)]
                halves.append(jnp.concatenate(two, axis=1))
            projected = jnp.concatenate(halves, axis=0) + p_cot
            z_part = thin(projected, m_high[...], ((1,), (0,)))
            z_part = z_part + mm(projected.astype(BF16), m_low[...])
            for j in range(PIECES):
                for e in range(NC):
                    zs[t, j * NC + e] = z_part[e * HALF : (e + 1) * HALF, j * LANES : (j + 1) * LANES]
        for o, e in group:
            send(
                zs.at[t, xs[o] * NC + cs[e]],
                zbuf1.at[t, g1],
                z1_send.at[t],
                z1_recv.at[t],
                (s, hid(xs[o], y, cs[e])),
            )
            send(
                zs.at[t, GROUP + ys[o] * NC + cs[e]],
                zbuf1.at[t, GROUP + g2],
                z1_send.at[t],
                z1_recv.at[t],
                (s, hid(x, ys[o], cs[e])),
            )
        zbuf1[t, g1] = zs[t, g1]
        zbuf1[t, GROUP + g2] = zs[t, GROUP + g2]
        if last:
            scatter_merged(chips[5:10])
        else:
            gather_rows(t + 1, chips[10:])
        with jax.named_scope("inverse"):
            gram = mm_high(projected, projected, ((1,), (1,)))
            inverse = inverse_lower(gram)
            new_left = mm_high(inverse, projected)
            if last:
                rows_f32[...] = new_left.T
                left_out[...] = rows_f32[pl.ds(pl.multiple_of(h * OWN, OWN), OWN), :]
            else:
                ls[t, :, :ROWS] = new_left
                ls[t, :, ROWS:] = jnp.concatenate([inverse, jnp.zeros((RANK, LANES - RANK), F32)], axis=1)
        if not last:

            @pl.when(has_below)
            def _():
                send(ls.at[t], lz.at[t], l_send.at[t], l_recv.at[t], (s - 1, h))

        with jax.named_scope("z_cot"):
            mix = mm_high(projected, l_f32[...], ((1,), (1,)))
            for k, place in enumerate((x, NX + y)):
                lanes = pl.ds(pl.multiple_of(place * LANES, LANES), LANES)
                z_cot = mm_high(mix, r_f32[:, lanes])
                for e in range(NC):
                    zc[k, e] = z_cot[e * HALF : (e + 1) * HALF, :]
        drain(zbuf1.at[t, pl.ds(0, 2 * (GROUP - 1))], z1_recv.at[t], "z1_recv")
        first = total(zbuf1, t, 0, GROUP)
        second = total(zbuf1, t, GROUP, GROUP)
        zs1[t, 0] = first
        zs1[t, 1] = second
        for o in far:
            send(
                zs1.at[t, 0],
                zbuf2.at[t, y],
                z2_send.at[t],
                z2_recv.at[t],
                (s, hid(x, ys[o], c)),
            )
            send(
                zs1.at[t, 1],
                zbuf2.at[t, NY + x],
                z2_send.at[t],
                z2_recv.at[t],
                (s, hid(xs[o], y, c)),
            )
        zbuf2[t, y] = first
        zbuf2[t, NY + x] = second
        if not last:
            share_rows(t + 1)
            make_mask(t + 1)
        else:
            scatter_merged(chips[10:])
            with jax.named_scope("cot_rows"):
                rows_f32[...] = l_f32[...].T
                own_left = rows_f32[pl.ds(pl.multiple_of(h * OWN, OWN), OWN), :]
                merged = mm_high(own_left, r_f32[...])
        drain(zbuf2.at[t, pl.ds(0, 2 * (NY - 1))], z2_recv.at[t], "z2_recv")
        with jax.named_scope("r_piece"):
            first = total(zbuf2, t, 0, NY) + zc[0, c]
            second = total(zbuf2, t, NY, NX) + zc[1, c]
            zp[t, 0] = first
            zp[t, 1] = second
        slots = (g1, GROUP + g2)
        if not last:

            @pl.when(has_below)
            def _():
                for i in (2, 1, 3, 0):
                    for e in range(NC):
                        for k, place in enumerate((hid(xs[i], y, cs[e]), hid(x, ys[i], cs[e]))):
                            send(
                                zp.at[t, k],
                                rzbuf.at[t, slots[k]],
                                rz_send.at[t],
                                rz_recv.at[t],
                                (s - 1, place),
                            )

        for o, e in group:
            for k, place in enumerate((hid(xs[o], y, cs[e]), hid(x, ys[o], cs[e]))):
                send(
                    zp.at[t, k],
                    rbuf.at[t, slots[k]],
                    r_send.at[t],
                    r_recv.at[t],
                    (s, place),
                )
        rbuf[t, g1] = first
        rbuf[t, GROUP + g2] = second

    t = TICKS - 1
    drain(mbuf.at[pl.ds(0, CHIPS - 1)], m_recv.at[1], "m_recv")
    for k in range(CHIPS):
        merged = merged + mbuf[k].astype(F32)
    grads_out[...] = merged
    drain(rbuf.at[t, pl.ds(0, 2 * (GROUP - 1))], r_recv.at[t], "r_recv")
    right_out[...] = times(inverse, unpack(rbuf, t))

    drain(msend.at[0], m_send.at[0])
    drain(mbuf.at[pl.ds(0, CHIPS - 1)], m_send.at[1])
    for t in range(TICKS):
        drain(x_full.at[t, pl.ds(0, CHIPS - 1), 0], ag_send.at[t])
        drain(x_full.at[t, :, 0], agp_send.at[t])
        drain(pbuf1.at[t, pl.ds(0, 2 * (GROUP - 1))], p1_send.at[t])
        drain(pbuf2.at[t, pl.ds(0, 2 * (GROUP - 1))], p2_send.at[t])
        drain(zbuf1.at[t, pl.ds(0, 2 * (GROUP - 1))], z1_send.at[t])
        drain(zbuf2.at[t, pl.ds(0, 2 * (NY - 1))], z2_send.at[t])
        drain(rbuf.at[t, pl.ds(0, 2 * (GROUP - 1))], r_send.at[t])
        if t + 1 < TICKS:

            @pl.when(has_below)
            def _():
                drain(rzbuf.at[t], rz_send.at[t])
                drain(lz.at[t], l_send.at[t])


def hand_over(merged_in, left_in, right_in, merged_out, left_out, right_out):
    merged_out[...] = merged_in[...]
    left_out[...] = left_in[...]
    right_out[...] = right_in[...]


def body(
    section_inputs,
    w_in,
    w_out,
    warm_factor,
    pending_left,
    pending_right,
    incoming_left,
    incoming_right,
):
    width = w_in.shape[2]
    dma = pltpu.SemaphoreType.DMA
    anywhere = pl.BlockSpec(memory_space=pltpu.MemorySpace.HBM)
    inside = pl.BlockSpec(memory_space=pltpu.VMEM)
    results = (
        jax.ShapeDtypeStruct((OWN, D), F32),
        jax.ShapeDtypeStruct((OWN, RANK), F32),
        jax.ShapeDtypeStruct((RANK, D), F32),
    )
    found = pl.pallas_call(
        kernel,
        out_shape=tuple(pltpu.VMEM(r.shape, r.dtype) for r in results),
        in_specs=[anywhere] * 8,
        out_specs=(inside, inside, inside),
        scratch_shapes=[
            pltpu.VMEM((D, width), BF16),
            pltpu.VMEM((width, D), BF16),
            pltpu.VMEM((TICKS, CHIPS, NC, OWN, D), BF16),
            pltpu.VMEM((ROWS, width), BF16),
            pltpu.VMEM((ROWS, width), BF16),
            pltpu.VMEM((RANK, ROWS), F32),
            pltpu.VMEM((RANK, D), F32),
            pltpu.VMEM((RANK, D), F32),
            pltpu.VMEM((TICKS, RANK, ROWS), F32),
            pltpu.VMEM((TICKS, RANK, D), F32),
            pltpu.VMEM((TICKS, NC, 2, HALF, LANES), F32),
            pltpu.VMEM((TICKS, 2 * GROUP, HALF, LANES), F32),
            pltpu.VMEM((TICKS, 2, HALF, LANES), F32),
            pltpu.VMEM((TICKS, 2 * GROUP, HALF, LANES), F32),
            pltpu.VMEM((TICKS, 2 * GROUP, HALF, LANES), F32),
            pltpu.VMEM((TICKS, 2 * GROUP, HALF, LANES), F32),
            pltpu.VMEM((TICKS, 2, HALF, LANES), F32),
            pltpu.VMEM((TICKS, NY + NX, HALF, LANES), F32),
            pltpu.VMEM((2, NC, HALF, LANES), F32),
            pltpu.VMEM((TICKS, 2, HALF, LANES), F32),
            pltpu.VMEM((RANK, D), F32),
            pltpu.VMEM((RANK, ROWS), F32),
            pltpu.VMEM((ROWS, D), BF16),
            pltpu.VMEM((ROWS, D), BF16),
            pltpu.VMEM((TICKS, 2 * GROUP, HALF, LANES), F32),
            pltpu.VMEM((TICKS, 2 * GROUP, HALF, LANES), F32),
            pltpu.VMEM((TICKS, RANK, ROWS + LANES), F32),
            pltpu.VMEM((TICKS, RANK, ROWS + LANES), F32),
            pltpu.VMEM((ROWS, RANK), F32),
            pltpu.VMEM((ROWS, D), F32),
            pltpu.VMEM((NC, CHIPS, OWN, D), BF16),
            pltpu.VMEM((CHIPS, OWN, D), BF16),
            pltpu.VMEM((CHIPS, OWN, D), BF16),
            pltpu.VMEM((CHIPS, OWN, D), BF16),
            dma((7,)),
        ]
        + [dma((TICKS,)), dma((TICKS, NX))]
        + [dma((TICKS,))] * 16
        + [dma((2,))] * 2,
        compiler_params=pltpu.CompilerParams(
            collective_id=0, has_side_effects=True, vmem_limit_bytes=66781184
        ),
    )(
        section_inputs[0],
        w_in[0],
        w_out[0],
        jnp.swapaxes(warm_factor[0], 0, 1),
        jnp.swapaxes(pending_left[0], 0, 1),
        jnp.swapaxes(pending_right[0], 0, 1),
        jnp.swapaxes(incoming_left, 1, 2),
        jnp.swapaxes(incoming_right, 1, 2),
    )
    merged, left, right = pl.pallas_call(
        hand_over,
        out_shape=results,
        in_specs=[inside] * 3,
        out_specs=(inside,) * 3,
        compiler_params=pltpu.CompilerParams(vmem_limit_bytes=1024 * 1024),
    )(*found)
    return (merged[None], left[None], jnp.swapaxes(right, 0, 1)[None])


def solution(mesh):
    placed = (
        P("pipe", None, "hid", None),
        P("pipe", None, "hid"),
        P("pipe", "hid", None),
        P("pipe", None, None),
        P("pipe", None, None),
        P("pipe", None, None),
        P(),
        P(),
    )
    return jax.shard_map(
        body,
        mesh=mesh,
        in_specs=placed,
        out_specs=(P("pipe", "hid", None), P("pipe", "hid", None), P("pipe", None, None)),
        check_vma=False,
    )
```
